32 devices in a mesh: row: 4 (over z), col: 8 (over y, x, core).
Axes of the slice: x: 2, y: 2, z: 4, core: 2. Of those that a mesh axis runs over, the one named last changes fastest.
Arguments:
- orbitals: bfloat16 [16, 64, 512], P('row', 'col'), may hold values from -6 to 6
- screened: bfloat16 [8192, 512], P(('row', 'col')), may hold values from -3.0517578e-05 to 3.0517578e-05
- kpoints: int32 [16], replicated, may hold values from 0 to 15, each once
- vectors: bfloat16 [64, 16384], P(None, ('row', 'col')), may hold values from -6 to 6
- energies: float32 [16, 64], replicated, may hold values from -1 to 1
Outputs:
- filtered: float32 [64, 16384], P(None, ('row', 'col'))
The draws below stay inside these ranges and needn't reach their ends.
All inputs are finite; a program needn't handle non-finite values.
Results may differ from the reference program's by a relative error of at most 0.0034.
Values may be sent and summed in bfloat16 or wider, within the bound.
No kernel may reach another device: no remote copies, remote signals or barrier semaphores. Data moves between devices by JAX's collectives and lax.ppermute only.
A program may use at most 128 MiB of HBM per device.

```python
import jax
import jax.numpy as jnp
from jax import lax

NV = 32
NC = 32
NG = 512
NX = 64
NK = 16
NB = 64


def draw_screened(key, part):
    spread_value = 0.5 / (NG * (NK * NV * NC) ** 0.5)
    values = jnp.clip(jax.random.normal(key, (NK * NG, NG), jnp.float32), -4.0, 4.0)
    return (values * spread_value).astype(jnp.bfloat16)


def steps_of(stream_key, dims, shards, low, largest):
    factor_of = 1.0
    for axis_at, blocks in shards:
        heights = jax.random.uniform(jax.random.fold_in(jax.random.fold_in(stream_key, 6), axis_at), (blocks,), jnp.float32, low / len(shards), largest / len(shards))
        factor_of = factor_of * jnp.repeat(jnp.exp(heights), dims[axis_at] // blocks).reshape((-1,) + (1,) * (len(dims) - 1 - axis_at))
    return factor_of


def bell_draw(rng, extent, width, limit, shards=(), kind=jnp.bfloat16):
    result = width * jax.random.normal(rng, extent, jnp.float32)
    if shards:
        result = result * steps_of(rng, extent, shards, -0.22, 0.18)
    return jnp.clip(result, -limit, limit).astype(kind)


def setup_inputs(seed: int = 0) -> dict:
    keys = jax.random.split(jax.random.key(seed), 6)
    return {
        "orbitals": bell_draw(keys[0], (NK, NB, NG), 1.0, 6.0, ((0, 4), (1, 8))),
        "screened": draw_screened(jax.random.fold_in(keys[5], 71), 0),
        "kpoints": jax.random.permutation(keys[2], NK).astype(jnp.int32),
        "vectors": bell_draw(keys[3], (NX, NK * NV * NC), 1.0, 6.0, ((1, 32),)),
        "energies": jnp.clip(jax.random.uniform(keys[4], (NK, NB), jnp.float32, -1.0, 1.0), -1.0, 1.0),
    }


SPREAD = 4.0


def pair_tile(orbit_left, orbit_right, screen_block):
    valence = orbit_left[:NV].astype(jnp.float32)[:, None, :] * orbit_right[:NV].astype(jnp.float32)[None, :, :]
    conduct = orbit_left[NV:].astype(jnp.float32)[:, None, :] * orbit_right[NV:].astype(jnp.float32)[None, :, :]
    valence = valence.reshape(NV * NV, NG).astype(jnp.bfloat16)
    conduct = conduct.reshape(NC * NC, NG).astype(jnp.bfloat16)
    amplitude = jnp.dot(valence, screen_block, preferred_element_type=jnp.float32).astype(jnp.bfloat16)
    inner_tile = jnp.dot(amplitude, conduct.T, preferred_element_type=jnp.float32)
    inner_tile = inner_tile.reshape(NV, NV, NC, NC).transpose(0, 2, 1, 3)
    return inner_tile.reshape(NV * NC, NV * NC).astype(jnp.bfloat16)


def apply_kernel(orbitals, screened, kpoints, rounded):
    shaped = rounded.reshape(NX, NK, NV * NC)

    def row_apply(left_index):
        def column_step(running, right_index):
            momentum = ((kpoints[left_index] - kpoints[right_index] + NK) % NK).astype(jnp.int32)
            screen_block = lax.dynamic_slice_in_dim(screened, momentum * NG, NG, 0)
            tile_value = pair_tile(orbitals[left_index], orbitals[right_index], screen_block)
            column = lax.dynamic_index_in_dim(shaped, right_index, 1, keepdims=False)
            return running + jnp.dot(column, tile_value.T, preferred_element_type=jnp.float32), None

        running, unused = lax.scan(column_step, jnp.zeros((NX, NV * NC), jnp.float32), jnp.arange(NK, dtype=jnp.int32))
        return running

    stacked = lax.map(row_apply, jnp.arange(NK, dtype=jnp.int32))
    return stacked.transpose(1, 0, 2).reshape(NX, NK * NV * NC)


def reference(orbitals, screened, kpoints, vectors, energies):
    gap_full = (energies[:, NV:][:, None, :] - energies[:, :NV][:, :, None]).reshape(NK * NV * NC)

    def hamilton(current, rounded):
        return (gap_full * current + apply_kernel(orbitals, screened, kpoints, rounded)) / SPREAD

    state_first = vectors.astype(jnp.float32)
    second = hamilton(state_first, vectors)
    state_third = 2.0 * hamilton(second, second.astype(jnp.bfloat16)) - state_first
    return 2.0 * hamilton(state_third, state_third.astype(jnp.bfloat16)) - second
```

```python
import functools

import jax
import jax.numpy as jnp
from jax import lax
from jax.experimental import pallas as pl
from jax.experimental.pallas import tpu as pltpu
from jax.sharding import PartitionSpec as P

NV = 32
NC = 32
NG = 512
SPREAD = 4.0
LANES = 128
AXES = ("row", "col")


def swap_groups(parts, lane):
    low_half = (lane // (2 * NC)) % 2 == 0
    low_pair = (lane // NC) % 2 == 0
    a0, a1, a2, a3 = parts
    roll = functools.partial(pltpu.roll, axis=1)
    p0 = jnp.where(low_half, a0, roll(a2, 2 * NC))
    p2 = jnp.where(low_half, roll(a0, 2 * NC), a2)
    p1 = jnp.where(low_half, a1, roll(a3, 2 * NC))
    p3 = jnp.where(low_half, roll(a1, 2 * NC), a3)
    b0 = jnp.where(low_pair, p0, roll(p1, NC))
    b1 = jnp.where(low_pair, roll(p0, 3 * NC), p1)
    b2 = jnp.where(low_pair, p2, roll(p3, NC))
    b3 = jnp.where(low_pair, roll(p2, 3 * NC), p3)
    return b0, b1, b2, b3


def tile_kernel(count, share, table, ok_ref, ol_ref, olw_ref, *refs):
    screen_refs = refs[:count]
    out_ref = refs[-1]
    sub = table[0]
    part = NG // count
    amplitude = jnp.zeros((NV * share, NG), jnp.float32)
    for m in range(count):
        here = pl.ds(pl.multiple_of((sub ^ m) * part, part), part)
        left = ok_ref[0, :NV, here].astype(jnp.float32)
        right = olw_ref[0, :, here].astype(jnp.float32)
        valence = (left[:, None, :] * right[None, :, :]).astype(jnp.bfloat16)
        valence = valence.reshape(NV * share, part)
        amplitude = amplitude + jnp.dot(
            valence, screen_refs[m][0], preferred_element_type=jnp.float32
        )
    amplitude = amplitude.astype(jnp.bfloat16)
    left = ok_ref[0, NV:, :].astype(jnp.float32)
    right = ol_ref[0, NV:, :].astype(jnp.float32)
    group = LANES // NC
    step = 2 * group
    moved = jnp.bfloat16 if share % 16 == 0 else jnp.float32
    lane = lax.broadcasted_iota(jnp.int32, (share, LANES), 1)
    for d0 in range(0, NC, step):
        conduct = (right[d0 : d0 + step][:, None, :] * left[None, :, :]).astype(jnp.bfloat16)
        conduct = conduct.reshape(step * NC, NG)
        tile = lax.dot_general(
            amplitude, conduct, (((1,), (1,)), ((), ())), preferred_element_type=jnp.float32
        )
        tile = tile.astype(moved)
        for d1 in range(0, step, group):
            for v0 in range(0, NV, group):
                parts = [
                    tile[(v0 + i) * share : (v0 + i + 1) * share, d1 * NC : d1 * NC + LANES]
                    for i in range(group)
                ]
                outs = jnp.concatenate(swap_groups(parts, lane), axis=0)
                out_ref[
                    0, (d0 + d1) * share : (d0 + d1 + group) * share, v0 * NC : v0 * NC + LANES
                ] = outs.astype(jnp.bfloat16)


def build_tiles(orbits, parts, table, total, first, share, before):
    count = len(parts)
    number = parts[0].shape[0]
    rows = NC * share
    in_specs = [
        pl.BlockSpec((1, NV + NC, NG), lambda j, t: (t[1], 0, 0)),
        pl.BlockSpec((1, NV + NC, NG), lambda j, t: (t[2 + j], 0, 0)),
        pl.BlockSpec((1, share, NG), lambda j, t: (t[2 + j], t[0], 0)),
    ]
    in_specs += [pl.BlockSpec((1, NG // count, NG), lambda j, t: (j, 0, 0))] * count
    operands = [orbits, orbits, orbits, *parts]
    aliases = {}
    if before is not None:
        in_specs.append(pl.BlockSpec(memory_space=pl.ANY))
        operands.append(before)
        aliases = {len(operands): 0}
    flops = 2 * number * NV * share * NG * (NG + NC * NC)
    return pl.pallas_call(
        functools.partial(tile_kernel, count, share),
        out_shape=jax.ShapeDtypeStruct((total, rows, NV * NC), jnp.bfloat16),
        grid_spec=pltpu.PrefetchScalarGridSpec(
            num_scalar_prefetch=1,
            grid=(number,),
            in_specs=in_specs,
            out_specs=pl.BlockSpec((1, rows, NV * NC), lambda j, t: (first + j, 0, 0)),
        ),
        input_output_aliases=aliases,
        cost_estimate=pl.CostEstimate(
            flops=flops, bytes_accessed=number * rows * NV * NC * 2, transcendentals=0
        ),
        name=f"tiles_{first}",
    )(table, *operands)


DEPTH = 4


def apply_kernel(shapes, count, table, tiles_ref, *refs):
    pieces = refs[: len(shapes)]
    outs = refs[len(shapes) : len(shapes) + count]
    buffer, total, sems = refs[len(shapes) + count :]
    where = [(p, s) for p, n in enumerate(shapes) for s in range(n)]

    def fetch(i):
        return pltpu.make_async_copy(
            tiles_ref.at[table[1 + i]], buffer.at[i % DEPTH], sems.at[i % DEPTH]
        )

    for i in range(min(DEPTH, len(where))):
        fetch(i).start()
    for i, (p, s) in enumerate(where):
        fetch(i).wait()
        part = jnp.dot(pieces[p][s], buffer[i % DEPTH], preferred_element_type=jnp.float32)
        if i == 0:
            total[...] = part
        else:
            total[...] += part
        if i + DEPTH < len(where):
            fetch(i + DEPTH).start()
    width = total.shape[1] // count
    for m in range(count):
        here = pl.ds(pl.multiple_of((table[0] ^ m) * width, width), width)
        outs[m][...] = total[:, here]


def apply_tiles(tiles, pieces, table, count):
    shapes = [p.shape[0] for p in pieces]
    vectors = pieces[0].shape[1]
    width = tiles.shape[2]
    whole = lambda p: pl.BlockSpec(memory_space=pltpu.VMEM)
    return pl.pallas_call(
        functools.partial(apply_kernel, shapes, count),
        out_shape=[jax.ShapeDtypeStruct((vectors, width // count), jnp.float32)] * count,
        in_specs=[pl.BlockSpec(memory_space=pltpu.SMEM), pl.BlockSpec(memory_space=pl.ANY)]
        + [whole(p) for p in pieces],
        out_specs=[pl.BlockSpec(memory_space=pltpu.VMEM)] * count,
        scratch_shapes=[
            pltpu.VMEM((DEPTH, *tiles.shape[1:]), jnp.bfloat16),
            pltpu.VMEM((vectors, width), jnp.float32),
            pltpu.SemaphoreType.DMA((DEPTH,)),
        ],
        cost_estimate=pl.CostEstimate(
            flops=2 * vectors * tiles.size, bytes_accessed=2 * tiles.size, transcendentals=0
        ),
        name="apply",
    )(table, tiles, *pieces)


def per_device(sizes, orbitals, screened, kpoints, vectors, energies):
    row_count, col_count = sizes
    points = kpoints.shape[0]
    count = row_count * col_count // points
    groups = col_count // count
    share = NV // count
    row = lax.axis_index("row")
    col = lax.axis_index("col")
    group, sub = col // count, col % count
    own = row * groups + group

    def send(array, move):
        pairs = []
        for r in range(row_count):
            for c in range(col_count):
                r2, g2, s2 = move(r, c // count, c % count)
                pairs.append((r * col_count + c, r2 * col_count + g2 * count + s2))
        return lax.ppermute(array, AXES, pairs)

    def along_row(array, s):
        return send(array, lambda r, g, u: ((r + s) % row_count, g, u))

    def along_group(array, e):
        return send(array, lambda r, g, u: (r, g ^ e, u))

    def along_sub(array, m):
        return send(array, lambda r, g, u: (r, g, u ^ m))

    row_orbits = lax.all_gather(orbitals, "col", axis=1, tiled=True)
    piece = groups // count
    mine = lax.dynamic_slice_in_dim(row_orbits, sub * piece, piece, 0)
    far = jnp.concatenate([along_row(mine, s) for s in range(1, row_count)], axis=0)
    orbits = jnp.concatenate(
        [row_orbits, far, *[along_sub(far, m) for m in range(1, count)]], axis=0
    )
    slot_points = [row * groups + i for i in range(groups)]
    for m in range(count):
        for s in range(1, row_count):
            for i in range(piece):
                slot_points.append((row - s) % row_count * groups + (sub ^ m) * piece + i)
    slot_points = jnp.stack(slot_points).astype(jnp.int32)

    numbers = jnp.arange(points, dtype=jnp.int32)
    block_at = jnp.stack(
        [
            (row - s) % row_count * groups + (group ^ e)
            for e in range(groups)
            for s in range(row_count)
        ]
    ).astype(jnp.int32)
    here = jnp.sum(jnp.where(numbers == own, kpoints, 0))
    wanted = (here - block_at + points) % points
    right = jnp.sum(jnp.where(kpoints[None, :] == wanted[:, None], numbers[None, :], 0), axis=1)
    right_slot = jnp.sum(
        jnp.where(slot_points[None, :] == right[:, None], numbers[None, :], 0), axis=1
    )
    tile_of = jnp.sum(
        jnp.where(block_at[:, None] == right[None, :], numbers[None, :], 0), axis=1
    )
    head = jnp.stack([sub, group]).astype(jnp.int32)
    tile_tables = [
        jnp.concatenate([head, right_slot[e * row_count : (e + 1) * row_count]])
        for e in range(groups)
    ]
    apply_table = jnp.concatenate([head[:1], tile_of])

    local = vectors.shape[1]
    place = jnp.arange(local, dtype=jnp.int32)
    source = (place % share) * NC + place // share
    order = (jnp.arange(local, dtype=jnp.int32)[:, None] == source[None, :]).astype(jnp.bfloat16)

    def gathered(rounded):
        turned = jnp.dot(rounded, order, preferred_element_type=jnp.float32).astype(jnp.bfloat16)
        line = jnp.stack([turned, *[along_row(turned, s) for s in range(1, row_count)]])
        return [line, *[along_group(line, e) for e in range(1, groups)]]

    first_pieces = gathered(vectors)

    line = jnp.stack([screened, *[along_row(screened, s) for s in range(1, row_count)]])
    tiles = None
    for e in range(groups):
        block = line if e == 0 else along_group(line, e)
        parts = [block, *[along_sub(block, m) for m in range(1, count)]]
        tiles = build_tiles(
            orbits, parts, tile_tables[e], points, e * row_count, share, tiles
        )

    gap_full = energies[:, NV:][:, None, :] - energies[:, :NV][:, :, None]
    gap_here = lax.dynamic_slice_in_dim(
        gap_full.reshape(points * NV * NC), (row * col_count + col) * local, local, 0
    )

    def hamilton(current, pieces):
        partial = apply_tiles(tiles, pieces, apply_table, count)
        product = partial[0]
        for m in range(1, count):
            product = product + along_sub(partial[m], m)
        return (gap_here * current + product) / SPREAD

    state_first = vectors.astype(jnp.float32)
    second = hamilton(state_first, first_pieces)
    third = 2.0 * hamilton(second, gathered(second.astype(jnp.bfloat16))) - state_first
    return 2.0 * hamilton(third, gathered(third.astype(jnp.bfloat16))) - second


def solution(mesh):
    placed = (P("row", "col", None), P(AXES, None), P(), P(None, AXES), P())
    sizes = (mesh.shape["row"], mesh.shape["col"])
    return jax.shard_map(
        functools.partial(per_device, sizes),
        mesh=mesh,
        in_specs=placed,
        out_specs=P(None, AXES),
        check_vma=False,
    )
```
